32 devices in a mesh: wide: 8 (over z, y), narrow: 4 (over x, core).
Axes of the slice: x: 2, y: 2, z: 4, core: 2. Of those that a mesh axis runs over, the one named last changes fastest.
Arguments:
- panel: float32 [16384, 128], P(('wide', 'narrow')), may hold values from -40 to 40
- trailing: float32 [16384, 256], P(('wide', 'narrow')), may hold values from -40 to 40
Outputs:
- q_factor: float32 [16384, 128], P(('wide', 'narrow'))
- r_factor: float32 [128, 128], replicated
- projection: float32 [128, 256], replicated
- updated: float32 [16384, 256], P(('wide', 'narrow'))
The draws below stay inside these ranges and needn't reach their ends.
All inputs are finite; a program needn't handle non-finite values.
Results may differ from the reference program's by a relative error of at most 0.00045.
Values sent between devices are 32-bit elements; how exact they have to be, the bound alone decides.
No kernel may reach another device: no remote copies, remote signals or barrier semaphores. Data moves between devices by JAX's collectives and lax.ppermute only.
A program may use at most 64 MiB of HBM per device.

```python
import math
import jax
import jax.numpy as jnp
from jax import lax

PANEL = 128
TRAIL = 256
ROWS = 16384


def design_parts(key):
    keys = jax.random.split(key, 8)
    factor_count = 4
    place = jnp.arange(ROWS, dtype=jnp.float32) / ROWS
    row_base = jnp.exp(jax.random.uniform(keys[0], (ROWS,), jnp.float32, math.log(0.25), math.log(2.5)))
    latent = jnp.clip(jax.random.normal(keys[1], (ROWS, factor_count), jnp.float32), -3.0, 3.0)
    own_noise = jnp.clip(jax.random.normal(keys[2], (ROWS, PANEL), jnp.float32), -4.0, 4.0)
    row_scale = row_base * (0.5 + place)
    raw_loads = jax.random.normal(keys[3], (factor_count, PANEL), jnp.float32)
    loadings = raw_loads / jnp.sum(jnp.abs(raw_loads), axis=0, keepdims=True)
    spread = jnp.exp(jax.random.uniform(keys[6], (PANEL,), jnp.float32, math.log(0.003), math.log(0.03)))
    column_scale = jnp.exp(jax.random.uniform(keys[7], (PANEL,), jnp.float32, math.log(0.3), math.log(3.0)))
    shared = jnp.dot(latent, loadings, precision=lax.Precision.HIGHEST)
    values = shared + own_noise * spread[None, :]
    panel = values * row_scale[:, None] * column_scale[None, :]
    panel = jnp.clip(panel, -40.0, 40.0)
    mixing = jax.random.normal(keys[4], (PANEL, TRAIL), jnp.float32) / math.sqrt(PANEL)
    noise_part = jax.random.normal(keys[5], (ROWS, TRAIL), jnp.float32) * (0.5 + place)[:, None]
    trailing = 0.5 * jnp.dot(panel, mixing, precision=lax.Precision.HIGHEST) + noise_part
    trailing = jnp.clip(trailing, -40.0, 40.0)
    return (panel, trailing)


def draw_panel(key, part):
    return design_parts(jax.random.fold_in(key, 11))[0]


def draw_trailing(key, part):
    return design_parts(jax.random.fold_in(key, 11))[1]


def setup_inputs(seed: int = 0) -> dict:
    key_of = jax.random.split(jax.random.key(seed), 3)
    panel = draw_panel(jax.random.fold_in(key_of[2], 71), 0)
    trailing = draw_trailing(jax.random.fold_in(key_of[2], 71), 0)
    return dict(panel=panel, trailing=trailing)


def upper_factor(gram_matrix):
    order = gram_matrix.shape[0]
    columns = jnp.arange(order, dtype=jnp.int32)

    def column_step(index, state):
        work, factor = state
        where = jnp.asarray(index).astype(jnp.int32)
        pivot_row = lax.dynamic_index_in_dim(work, where, 0, keepdims=False)
        pivot = lax.dynamic_index_in_dim(pivot_row, where, 0, keepdims=False)
        new_row = jnp.where(columns >= where, pivot_row / jnp.sqrt(pivot), jnp.zeros_like(pivot_row))
        work = work - new_row[:, None] * new_row[None, :]
        factor = lax.dynamic_update_slice_in_dim(factor, new_row[None, :], where, 0)
        return (work, factor)
    start = (gram_matrix, jnp.zeros_like(gram_matrix))
    return lax.fori_loop(0, order, column_step, start)[1]

def inverse_upper(upper_part):
    order = upper_part.shape[0]
    identity = jnp.eye(order, dtype=upper_part.dtype)

    def row_step(count, inverse):
        where = (order - 1 - jnp.asarray(count)).astype(jnp.int32)
        upper_row = lax.dynamic_index_in_dim(upper_part, where, 0, keepdims=False)
        unit_row = lax.dynamic_index_in_dim(identity, where, 0, keepdims=False)
        pivot = lax.dynamic_index_in_dim(upper_row, where, 0, keepdims=False)
        partial_value = jnp.dot(upper_row, inverse, precision=lax.Precision.HIGHEST)
        new_row = (unit_row - partial_value) / pivot
        return lax.dynamic_update_slice_in_dim(inverse, new_row[None, :], where, 0)
    return lax.fori_loop(0, order, row_step, jnp.zeros_like(upper_part))

def product(left, right):
    return jnp.dot(left, right, precision=lax.Precision.HIGHEST, preferred_element_type=jnp.float32)

def reference(panel, trailing):
    row_total = jnp.float32(ROWS)
    gram_first = product(panel.T, panel) / row_total
    first_factor = upper_factor(gram_first)
    basis_rows = product(panel, inverse_upper(first_factor))
    gram_second = product(basis_rows.T, basis_rows) / row_total
    second_factor = upper_factor(gram_second)
    q_factor = product(basis_rows, inverse_upper(second_factor))
    r_factor = product(second_factor, first_factor)
    cross_terms = product(panel.T, trailing) / row_total
    projection = product(inverse_upper(r_factor).T, cross_terms)
    updated = trailing - product(q_factor, projection)
    return (q_factor, r_factor, projection, updated)
```

```python
import functools

import jax
import jax.numpy as jnp
from jax import lax
from jax.experimental import pallas as pl
from jax.experimental.pallas import tpu as pltpu
from jax.sharding import PartitionSpec as P

AXES = ("wide", "narrow")
SUBLANES = 8
GRAM_SLICES = 5
FACTOR_SLICES = 5
VMEM = pl.BlockSpec(memory_space=pltpu.VMEM)


def product(left, right, contract=(1, 0)):
    dims = (((contract[0],), (contract[1],)), ((), ()))
    return lax.dot_general(
        left, right, dims, precision=lax.Precision.HIGHEST, preferred_element_type=jnp.float32
    )


def exact_product(left, right, contract):
    dims = (((contract[0],), (contract[1],)), ((), ()))
    return lax.dot_general(left, right, dims, preferred_element_type=jnp.float32)


def two_sum(left, right):
    total = left + right
    shown = total - left
    return total, (left - (total - shown)) + (right - shown)


def fixed_point_slices(value, peak, first_bits, count):
    sigma = peak * float(2 ** (24 - first_bits))
    terms = []
    for _ in range(count):
        term = (value + sigma) - sigma
        value = value - term
        terms.append(term.astype(jnp.bfloat16))
        sigma = sigma * float(2.0 ** -(first_bits + 1))
    return terms


def gram_kernel(panel_ref, trailing_ref, out_ref):
    panel = panel_ref[...]
    peak = jnp.max(jnp.abs(panel), axis=0, keepdims=True)
    terms = fixed_point_slices(panel, peak, 7, GRAM_SLICES)
    dot = functools.partial(exact_product, contract=(0, 0))
    first = dot(terms[0], terms[0])
    second = dot(terms[0], terms[1])
    rest = dot(terms[0], terms[2])
    rest = rest + dot(terms[1], terms[2]) + dot(terms[0], terms[3])
    rest = rest + dot(terms[0], terms[4]) + dot(terms[1], terms[3])
    rest = rest + rest.T + dot(terms[1], terms[1]) + dot(terms[2], terms[2])
    second, second_low = two_sum(second, second.T)
    high, high_low = two_sum(first, second)
    high, low = two_sum(high, high_low + (second_low + rest))
    cross = product(panel, trailing_ref[...], (0, 0))
    groups = high.shape[0] // SUBLANES
    for group in range(groups):
        rows = slice(group * SUBLANES, (group + 1) * SUBLANES)
        out_ref[2 * group * SUBLANES : (2 * group + 1) * SUBLANES, :] = high[rows]
        out_ref[(2 * group + 1) * SUBLANES : (2 * group + 2) * SUBLANES, :] = low[rows]
    width = high.shape[1]
    for part in range(cross.shape[1] // width):
        base = (2 + part) * high.shape[0]
        out_ref[base : base + high.shape[0], :] = cross[:, part * width : (part + 1) * width]


def sum_kernel(is_gram_ref, parts_ref, out_ref):
    half = parts_ref.shape[1] // 2
    highs = [parts_ref[d, :half, :] for d in range(parts_ref.shape[0])]
    lows = [parts_ref[d, half:, :] for d in range(parts_ref.shape[0])]
    plain = lows
    while len(highs) > 1:
        pairs = [two_sum(highs[i], highs[i + 1]) for i in range(0, len(highs), 2)]
        plain = [plain[i] + plain[i + 1] for i in range(0, len(plain), 2)]
        lows = [lows[i] + lows[i + 1] for i in range(0, len(lows), 2)]
        lows = [low + pair[1] for low, pair in zip(lows, pairs)]
        highs = [pair[0] for pair in pairs]
    high, low = two_sum(highs[0], lows[0])
    gram = jnp.full(high.shape, is_gram_ref[0], jnp.int32) != 0
    first = jnp.where(gram, high, highs[0])
    second = jnp.where(gram, low, plain[0])
    for d in range(parts_ref.shape[0]):
        out_ref[d, :half, :] = first
        out_ref[d, half:, :] = second


def factor_and_inverse(tiles):
    count = len(tiles)
    shape = tiles[0].shape
    lane = lax.broadcasted_iota(jnp.int32, shape, 1)
    sub = lax.broadcasted_iota(jnp.int32, shape, 0)
    over_lanes = lambda v, c: jnp.broadcast_to(v[:, c : c + 1], shape)
    over_rows = lambda v, i: jnp.broadcast_to(v[i : i + 1, :], shape)
    tiles = list(tiles)
    upper, lower = [], []
    for t in range(count):
        base = t * SUBLANES
        current = tiles[t]
        columns = {
            s: [over_lanes(tiles[s], base + c) for c in range(SUBLANES)] for s in range(t, count)
        }
        inside = (lane >= base) & (lane < base + SUBLANES)
        for s in range(t + 1, count):
            tiles[s] = jnp.where(inside, 0.0, tiles[s])
        pivots = jnp.zeros(shape, jnp.float32)
        for i in range(SUBLANES):
            k = base + i
            pivot = over_rows(columns[t][i], i)
            inverse = 1.0 / pivot
            pivots = jnp.where(sub == i, pivot, pivots)
            row = jnp.where(lane == k, 1.0, over_rows(current, i))
            later = {c: over_rows(columns[t][c], i) for c in range(i + 1, SUBLANES)}
            below = jnp.where((lane > k) & (lane < base + SUBLANES), 0.0, row)
            for s in range(t, count):
                multiplier = columns[s][i] * inverse
                if s == t:
                    if i == SUBLANES - 1:
                        continue
                    multiplier = jnp.where(sub > i, multiplier, 0.0)
                    current = jnp.where((lane == k) & (sub > i), 0.0, current) - multiplier * row
                else:
                    tiles[s] = tiles[s] - multiplier * below
                for c in later:
                    columns[s][c] = columns[s][c] - multiplier * later[c]
        scale = lax.rsqrt(pivots)
        scaled = current * scale
        diagonal = sub + base
        upper.append(jnp.where(lane >= diagonal, scaled, 0.0))
        lower.append(jnp.where(lane < diagonal, scaled, jnp.where(lane == diagonal, scale, 0.0)))
    return jnp.concatenate(upper, 0), jnp.concatenate(lower, 0)


def row_blocks(matrix):
    return [matrix[i : i + SUBLANES] for i in range(0, matrix.shape[0], SUBLANES)]


def final_kernel(row_total, sums_ref, panel_ref, trailing_ref, q_ref, r_ref, p_ref, u_ref):
    order = panel_ref.shape[1]
    groups = order // SUBLANES
    inverse_rows = 1.0 / row_total
    pick = lambda j: sums_ref[j * SUBLANES : (j + 1) * SUBLANES, :] * inverse_rows
    high_tiles = [pick(2 * g) for g in range(groups)]
    high = jnp.concatenate(high_tiles, 0)
    low = jnp.concatenate([pick(2 * g + 1) for g in range(groups)], 0)
    first_factor, first_inverse_t = factor_and_inverse(high_tiles)

    peak = jnp.max(jnp.abs(first_factor), axis=0, keepdims=True)
    terms = fixed_point_slices(first_factor, peak, 8, FACTOR_SLICES)
    orders = []
    for size in range(1, FACTOR_SLICES + 1):
        left = jnp.concatenate(terms[:size], 0)
        right = jnp.concatenate(terms[:size][::-1], 0)
        orders.append(exact_product(left, right, (0, 0)))
    remainder, error = two_sum(high, -orders[0])
    remainder, error_next = two_sum(remainder, -orders[1])
    rest = low - orders[2]
    for term in orders[3:]:
        rest = rest - term
    remainder = remainder + ((error + error_next) + rest)
    near_one_t = product(first_inverse_t, first_factor, (1, 1))
    near_one = product(first_factor, first_inverse_t, (1, 1))
    carried = product(remainder, first_inverse_t, (1, 1))
    gram_second = product(
        jnp.concatenate([near_one_t, first_inverse_t], 1), jnp.concatenate([near_one, carried], 0)
    )
    second_factor, second_inverse_t = factor_and_inverse(row_blocks(gram_second))

    r_ref[...] = product(second_factor, first_factor)
    inverse_t = product(second_inverse_t, first_inverse_t)
    parts = (sums_ref.shape[0] - 2 * order) // order
    cross = jnp.concatenate(
        [sums_ref[(2 + j) * order : (3 + j) * order, :] * inverse_rows for j in range(parts)], 1
    )
    projection = product(inverse_t, cross)
    p_ref[...] = projection
    q_factor = product(panel_ref[...], inverse_t, (1, 1))
    q_ref[...] = q_factor
    u_ref[...] = trailing_ref[...] - product(q_factor, projection)


def call(body, outs, n_in, specs=None):
    return pl.pallas_call(
        body,
        out_shape=[jax.ShapeDtypeStruct(shape, jnp.float32) for shape in outs],
        in_specs=specs or [VMEM] * n_in,
        out_specs=[VMEM] * len(outs),
    )


def on_device(panel, trailing):
    rows, order = panel.shape
    width = trailing.shape[1]
    devices = lax.axis_size(AXES)
    row_total = float(rows * devices)
    total = 2 * order + order * width // order
    (local,) = call(gram_kernel, [(total, order)], 2)(panel, trailing)

    depth = total // (2 * devices)
    pieces = SUBLANES // depth
    slots = local.reshape(total // (2 * SUBLANES), 2, pieces, depth, order)
    slots = slots.transpose(0, 2, 1, 3, 4).reshape(devices, 2 * depth, order)
    parts = lax.all_to_all(slots, AXES, 0, 0)
    is_gram = (lax.axis_index(AXES) * 2 * depth < 2 * order).astype(jnp.int32).reshape(1)
    specs = [pl.BlockSpec(memory_space=pltpu.SMEM), VMEM]
    (summed,) = call(sum_kernel, [(devices, 2 * depth, order)], 2, specs)(is_gram, parts)
    sums = lax.all_to_all(summed, AXES, 0, 0)
    sums = sums.reshape(total // (2 * SUBLANES), pieces, 2, depth, order)
    sums = sums.transpose(0, 2, 1, 3, 4).reshape(total, order)

    outs = [(rows, order), (order, order), (order, width), (rows, width)]
    return tuple(call(functools.partial(final_kernel, row_total), outs, 3)(sums, panel, trailing))


def solution(mesh):
    in_specs = (P(AXES, None), P(AXES, None))
    out_specs = (P(AXES, None), P(), P(), P(AXES, None))
    return jax.shard_map(
        on_device, mesh=mesh, in_specs=in_specs, out_specs=out_specs, check_vma=False
    )
```

```python
import functools

import jax
import jax.numpy as jnp
from jax import lax
from jax.experimental import pallas as pl
from jax.experimental.pallas import tpu as pltpu
from jax.sharding import PartitionSpec as P

AXES = ("wide", "narrow")
SUBLANES = 8
GRAM_SLICES = 5
FACTOR_SLICES = 5
VMEM = pl.BlockSpec(memory_space=pltpu.VMEM)


def product(left, right, contract=(1, 0)):
    dims = (((contract[0],), (contract[1],)), ((), ()))
    return lax.dot_general(
        left, right, dims, precision=lax.Precision.HIGHEST, preferred_element_type=jnp.float32
    )


def exact_product(left, right, contract):
    dims = (((contract[0],), (contract[1],)), ((), ()))
    return lax.dot_general(left, right, dims, preferred_element_type=jnp.float32)


def two_sum(left, right):
    total = left + right
    shown = total - left
    return total, (left - (total - shown)) + (right - shown)


def fixed_point_slices(value, peak, first_bits, count):
    sigma = peak * float(2 ** (24 - first_bits))
    terms = []
    for _ in range(count):
        term = (value + sigma) - sigma
        value = value - term
        terms.append(term.astype(jnp.bfloat16))
        sigma = sigma * float(2.0 ** -(first_bits + 1))
    return terms


def gram_kernel(panel_ref, trailing_ref, out_ref):
    panel = panel_ref[...]
    peak = jnp.max(jnp.abs(panel), axis=0, keepdims=True)
    terms = fixed_point_slices(panel, peak, 7, GRAM_SLICES)
    dot = functools.partial(exact_product, contract=(0, 0))
    first = dot(terms[0], terms[0])
    second = dot(terms[0], terms[1])
    rest = dot(terms[0], terms[2])
    rest = rest + dot(terms[1], terms[2]) + dot(terms[0], terms[3])
    rest = rest + dot(terms[0], terms[4]) + dot(terms[1], terms[3])
    rest = rest + rest.T + dot(terms[1], terms[1]) + dot(terms[2], terms[2])
    second, second_low = two_sum(second, second.T)
    high, high_low = two_sum(first, second)
    high, low = two_sum(high, high_low + (second_low + rest))
    cross = product(panel, trailing_ref[...], (0, 0))
    high_half, high_rest = pack_symmetric(high)
    low_half, low_rest = pack_symmetric(low)
    half = high_half.shape[0] // 2
    width = cross.shape[1] // 2
    for core in range(2):
        rows = slice(core * half, (core + 1) * half)
        blocks = [high_half[rows], high_rest, low_half[rows], low_rest]
        blocks.append(cross[:, core * width : (core + 1) * width])
        at = 0
        for block in blocks:
            out_ref[core, at : at + block.shape[0], :] = block
            at += block.shape[0]


def grid_of(shape):
    return (lax.broadcasted_iota(jnp.int32, shape, d) for d in range(2))


def pack_symmetric(matrix):
    order = matrix.shape[0]
    half = order // 2
    top = matrix[:half]
    bottom = pltpu.roll(matrix[half:], half, 1)
    row, lane = grid_of(top.shape)
    rest = jnp.sum(jnp.where(row == lane, bottom, 0.0), axis=0, keepdims=True)
    return jnp.where(lane < row, bottom, top), jnp.broadcast_to(rest, (SUBLANES, order))


def unpack_symmetric(packed, rest):
    half, order = packed.shape
    turned = packed.T
    left, right = packed[:, :half], packed[:, half:]
    row, lane = grid_of(left.shape)
    diagonal = jnp.broadcast_to(rest[:1, :half], left.shape)
    top = jnp.concatenate([jnp.where(lane >= row, left, turned[:half]), right], 1)
    lower = jnp.where(lane < row, left, jnp.where(lane == row, diagonal, turned[:half]))
    return jnp.concatenate([top, jnp.concatenate([turned[half:], lower], 1)], 0)


def add_terms(left, right, pair_rows):
    high, error = two_sum(left[:pair_rows], right[:pair_rows])
    low = (left[pair_rows : 2 * pair_rows] + right[pair_rows : 2 * pair_rows]) + error
    return jnp.concatenate([high, low, left[2 * pair_rows :] + right[2 * pair_rows :]], 0)


def factor_and_inverse(tiles):
    count = len(tiles)
    shape = tiles[0].shape
    lane = lax.broadcasted_iota(jnp.int32, shape, 1)
    sub = lax.broadcasted_iota(jnp.int32, shape, 0)
    over_lanes = lambda v, c: jnp.broadcast_to(v[:, c : c + 1], shape)
    over_rows = lambda v, i: jnp.broadcast_to(v[i : i + 1, :], shape)
    tiles = list(tiles)
    upper, lower = [], []
    for t in range(count):
        base = t * SUBLANES
        current = tiles[t]
        columns = {
            s: [over_lanes(tiles[s], base + c) for c in range(SUBLANES)] for s in range(t, count)
        }
        inside = (lane >= base) & (lane < base + SUBLANES)
        for s in range(t + 1, count):
            tiles[s] = jnp.where(inside, 0.0, tiles[s])
        pivots = jnp.zeros(shape, jnp.float32)
        for i in range(SUBLANES):
            k = base + i
            pivot = over_rows(columns[t][i], i)
            inverse = 1.0 / pivot
            pivots = jnp.where(sub == i, pivot, pivots)
            row = jnp.where(lane == k, 1.0, over_rows(current, i))
            later = {c: over_rows(columns[t][c], i) for c in range(i + 1, SUBLANES)}
            below = jnp.where((lane > k) & (lane < base + SUBLANES), 0.0, row)
            for s in range(t, count):
                multiplier = columns[s][i] * inverse
                if s == t:
                    if i == SUBLANES - 1:
                        continue
                    multiplier = jnp.where(sub > i, multiplier, 0.0)
                    current = jnp.where((lane == k) & (sub > i), 0.0, current) - multiplier * row
                else:
                    tiles[s] = tiles[s] - multiplier * below
                for c in later:
                    columns[s][c] = columns[s][c] - multiplier * later[c]
        scale = lax.rsqrt(pivots)
        scaled = current * scale
        diagonal = sub + base
        upper.append(jnp.where(lane >= diagonal, scaled, 0.0))
        lower.append(jnp.where(lane < diagonal, scaled, jnp.where(lane == diagonal, scale, 0.0)))
    return jnp.concatenate(upper, 0), jnp.concatenate(lower, 0)


def row_blocks(matrix):
    return [matrix[i : i + SUBLANES] for i in range(0, matrix.shape[0], SUBLANES)]


def final_kernel(row_total, core_ref, own_ref, other_ref, panel_ref, trailing_ref, q_ref, r_ref, p_ref, u_ref):
    order = panel_ref.shape[1]
    inverse_rows = 1.0 / row_total
    swapped = jnp.full(own_ref.shape, core_ref[0], jnp.int32) != 0
    own = own_ref[...] * inverse_rows
    other = other_ref[...] * inverse_rows
    halves = [jnp.where(swapped, other, own), jnp.where(swapped, own, other)]
    quarter = order // 4
    pair_rows = quarter + SUBLANES
    pick = lambda at: unpack_symmetric(
        jnp.concatenate([half[at : at + quarter] for half in halves], 0),
        halves[0][at + quarter : at + pair_rows],
    )
    high = pick(0)
    low = pick(pair_rows)
    cross = jnp.concatenate([half[2 * pair_rows :] for half in halves], 1)
    high_tiles = row_blocks(high)
    first_factor, first_inverse_t = factor_and_inverse(high_tiles)

    peak = jnp.max(jnp.abs(first_factor), axis=0, keepdims=True)
    terms = fixed_point_slices(first_factor, peak, 8, FACTOR_SLICES)
    orders = []
    for size in range(1, FACTOR_SLICES + 1):
        left = jnp.concatenate(terms[:size], 0)
        right = jnp.concatenate(terms[:size][::-1], 0)
        orders.append(exact_product(left, right, (0, 0)))
    remainder, error = two_sum(high, -orders[0])
    remainder, error_next = two_sum(remainder, -orders[1])
    rest = low - orders[2]
    for term in orders[3:]:
        rest = rest - term
    remainder = remainder + ((error + error_next) + rest)
    near_one_t = product(first_inverse_t, first_factor, (1, 1))
    near_one = product(first_factor, first_inverse_t, (1, 1))
    carried = product(remainder, first_inverse_t, (1, 1))
    gram_second = product(
        jnp.concatenate([near_one_t, first_inverse_t], 1), jnp.concatenate([near_one, carried], 0)
    )
    second_factor, second_inverse_t = factor_and_inverse(row_blocks(gram_second))

    r_ref[...] = product(second_factor, first_factor)
    inverse_t = product(second_inverse_t, first_inverse_t)
    projection = product(inverse_t, cross)
    p_ref[...] = projection
    q_factor = product(panel_ref[...], inverse_t, (1, 1))
    q_ref[...] = q_factor
    u_ref[...] = trailing_ref[...] - product(q_factor, projection)


def call(body, outs, n_in, specs=None, near=False):
    return pl.pallas_call(
        body,
        out_shape=[(pltpu.VMEM if near else jax.ShapeDtypeStruct)(shape, jnp.float32) for shape in outs],
        in_specs=specs or [VMEM] * n_in,
        out_specs=[VMEM] * len(outs),
    )


def all_sum(blocks, pair_rows):
    devices = lax.axis_size(AXES)
    bits = devices.bit_length() - 1
    send = lambda value, mask: lax.ppermute(value, AXES, [(i, i ^ mask) for i in range(devices)])
    add = functools.partial(add_terms, pair_rows=pair_rows)
    odd = lax.axis_index(AXES) % 2
    own = jnp.where(odd == 0, blocks[0], blocks[1])
    value = add(own, send(jnp.where(odd == 0, blocks[1], blocks[0]), 1))
    stages = [(bit,) for bit in range(3, bits)]
    stages.insert(1, (1, 2))
    for stage in stages:
        first = 1 << stage[0]
        if len(stage) == 1:
            value = add(value, send(value, first))
        else:
            second = 1 << stage[1]
            near, far, across = [send(value, mask) for mask in (first, second, first | second)]
            value = add(add(value, near), add(far, across))
    return value, send(value, 1), odd


def on_device(panel, trailing):
    rows, order = panel.shape
    width = trailing.shape[1]
    row_total = float(rows * lax.axis_size(AXES))
    pair_rows = order // 4 + SUBLANES
    (local,) = call(gram_kernel, [(2, 2 * pair_rows + order, order)], 2, near=True)(panel, trailing)
    own, other, odd = all_sum(local, pair_rows)
    outs = [(rows, order), (order, order), (order, width), (rows, width)]
    specs = [pl.BlockSpec(memory_space=pltpu.SMEM)] + [VMEM] * 4
    body = functools.partial(final_kernel, row_total)
    own, other = [pltpu.with_memory_space_constraint(v, pltpu.VMEM) for v in (own, other)]
    core = odd.astype(jnp.int32).reshape(1)
    return tuple(call(body, outs, 5, specs)(core, own, other, panel, trailing))


def solution(mesh):
    in_specs = (P(AXES, None), P(AXES, None))
    out_specs = (P(AXES, None), P(), P(), P(AXES, None))
    return jax.shard_map(
        on_device, mesh=mesh, in_specs=in_specs, out_specs=out_specs, check_vma=False
    )
```

```python
import functools

import jax
import jax.numpy as jnp
from jax import lax
from jax.experimental import pallas as pl
from jax.experimental.pallas import tpu as pltpu
from jax.sharding import PartitionSpec as P

AXES = ("wide", "narrow")
SUBLANES = 8
GRAM_SLICES = 5
FACTOR_SLICES = 4
OUTER = 4
CHUNKS = 4
VMEM = pl.BlockSpec(memory_space=pltpu.VMEM)


def matmul(left, right):
    return exact_product(left, right, (1, 0))


def bf16_terms(value, count):
    terms = []
    for _ in range(count):
        term = value.astype(jnp.bfloat16)
        value = value - term.astype(jnp.float32)
        terms.append(term)
    return terms


def wide(right):
    column = jnp.concatenate([right[0], right[1]], 1)
    return jnp.concatenate([column, column], 0)


def product_of_terms(left, right):
    columns = right[0].shape[1]
    small = matmul(jnp.concatenate([left[2], left[0]], 1), jnp.concatenate([right[0], right[2]], 0))
    both = matmul(jnp.concatenate(left[:2], 1), wide(right))
    return (small + both[:, columns:]) + both[:, :columns]


def product(left, right):
    return product_of_terms(bf16_terms(left, 3), bf16_terms(right, 3))


def exact_product(left, right, contract):
    dims = (((contract[0],), (contract[1],)), ((), ()))
    return lax.dot_general(left, right, dims, preferred_element_type=jnp.float32)


def two_sum(left, right):
    total = left + right
    shown = total - left
    return total, (left - (total - shown)) + (right - shown)


def fixed_point_slices(value, peak, first_bits, count):
    sigma = peak * float(2 ** (24 - first_bits))
    terms = []
    for _ in range(count):
        term = (value + sigma) - sigma
        value = value - term
        terms.append(term.astype(jnp.bfloat16))
        sigma = sigma * float(2.0 ** -(first_bits + 1))
    return terms


def gram_kernel(panel_ref, trailing_ref, out_ref):
    panel = panel_ref[...]
    peak = jnp.max(jnp.abs(panel), axis=0, keepdims=True)
    terms = fixed_point_slices(panel, peak, 7, GRAM_SLICES)
    dot = functools.partial(exact_product, contract=(0, 0))
    first = dot(terms[0], terms[0])
    second = dot(terms[0], terms[1])
    rest = dot(terms[0], terms[2])
    rest = rest + dot(terms[1], terms[2]) + dot(terms[0], terms[3])
    rest = rest + dot(terms[0], terms[4]) + dot(terms[1], terms[3])
    rest = rest + rest.T + dot(terms[1], terms[1]) + dot(terms[2], terms[2])
    second, second_low = two_sum(second, second.T)
    high, high_low = two_sum(first, second)
    high, low = two_sum(high, high_low + (second_low + rest))
    dims = (((0,), (0,)), ((), ()))
    cross = lax.dot_general(
        panel, trailing_ref[...], dims, precision=lax.Precision.HIGHEST, preferred_element_type=jnp.float32
    )
    high_half, high_rest = pack_symmetric(high)
    low_half, low_rest = pack_symmetric(low)
    half = high_half.shape[0] // 2
    width = cross.shape[1] // 2
    for core in range(2):
        rows = slice(core * half, (core + 1) * half)
        blocks = [high_half[rows], high_rest, low_half[rows], low_rest]
        blocks.append(cross[:, core * width : (core + 1) * width])
        at = 0
        for block in blocks:
            out_ref[core, at : at + block.shape[0], :] = block
            at += block.shape[0]


def grid_of(shape):
    return (lax.broadcasted_iota(jnp.int32, shape, d) for d in range(2))


def pack_symmetric(matrix):
    order = matrix.shape[0]
    half = order // 2
    top = matrix[:half]
    bottom = pltpu.roll(matrix[half:], half, 1)
    row, lane = grid_of(top.shape)
    rest = jnp.sum(jnp.where(row == lane, bottom, 0.0), axis=0, keepdims=True)
    return jnp.where(lane < row, bottom, top), jnp.broadcast_to(rest, (SUBLANES, order))


def unpack_symmetric(packed, rest):
    half, order = packed.shape
    turned = packed.T
    left, right = packed[:, :half], packed[:, half:]
    row, lane = grid_of(left.shape)
    diagonal = jnp.broadcast_to(rest[:1, :half], left.shape)
    top = jnp.concatenate([jnp.where(lane >= row, left, turned[:half]), right], 1)
    lower = jnp.where(lane < row, left, jnp.where(lane == row, diagonal, turned[:half]))
    return jnp.concatenate([top, jnp.concatenate([turned[half:], lower], 1)], 0)


def add_terms(left, right, pair_rows):
    high, error = two_sum(left[:pair_rows], right[:pair_rows])
    low = (left[pair_rows : 2 * pair_rows] + right[pair_rows : 2 * pair_rows]) + error
    return jnp.concatenate([high, low, left[2 * pair_rows :] + right[2 * pair_rows :]], 0)


def outer_update(rows, pivots):
    left, right = bf16_terms(rows, 3), bf16_terms(pivots, 3)
    left = [left[i] for i in (2, 1, 0, 1, 0, 0)]
    right = [right[i] for i in (0, 1, 2, 0, 1, 0)]
    return exact_product(jnp.concatenate(left, 0), jnp.concatenate(right, 0), (0, 0))


def factor_and_inverse(tiles):
    count = len(tiles)
    shape = tiles[0].shape
    sub, lane = grid_of(shape)
    over_lanes = lambda v, c: jnp.broadcast_to(v[:, c : c + 1], shape)
    over_rows = lambda v, i: jnp.broadcast_to(v[i : i + 1, :], shape)
    tiles = list(tiles)
    upper, lower = [], []
    for first in range(0, count, OUTER):
        last = min(first + OUTER, count)
        size = last - first
        start, stop = first * SUBLANES, last * SUBLANES
        columns = [
            [over_lanes(tiles[first + s], start + c) for c in range(SUBLANES * (s + 1))]
            for s in range(size)
        ]
        pivot_rows = []
        for t in range(size):
            base = start + t * SUBLANES
            current = tiles[first + t]
            inside = (lane >= base) & (lane < base + SUBLANES)
            for s in range(t + 1, size):
                tiles[first + s] = jnp.where(inside, 0.0, tiles[first + s])
            pivots = jnp.zeros(shape, jnp.float32)
            for i in range(SUBLANES):
                k = base + i
                own = t * SUBLANES + i
                pivot = over_rows(columns[t][own], i)
                inverse = 1.0 / pivot
                pivots = jnp.where(sub == i, pivot, pivots)
                row = jnp.where(lane == k, 1.0, over_rows(current, i))
                later = {
                    c: over_rows(columns[c // SUBLANES][own], c % SUBLANES)
                    for c in range(own + 1, SUBLANES * size)
                }
                if i < SUBLANES - 1:
                    column = jnp.where(sub > i, columns[t][own], 0.0)
                    for c in range(own + 1, SUBLANES * (t + 1)):
                        columns[t][c] = columns[t][c] - (column * later[c]) * inverse
                    kept = jnp.where((lane == k) & (sub > i), 0.0, current)
                    current = kept - (column * row) * inverse
                if t + 1 < size:
                    below = jnp.where((lane > k) & (lane < base + SUBLANES), 0.0, row) * inverse
                    scaled = {c: later[c] * inverse for c in later}
                    for s in range(t + 1, size):
                        column = columns[s][own]
                        tiles[first + s] = tiles[first + s] - column * below
                        for c in range(own + 1, SUBLANES * (s + 1)):
                            columns[s][c] = columns[s][c] - column * scaled[c]
            scale = lax.rsqrt(pivots)
            value = current * scale
            diagonal = sub + base
            upper.append(jnp.where(lane >= diagonal, value, 0.0))
            lower.append(jnp.where(lane < diagonal, value, jnp.where(lane == diagonal, scale, 0.0)))
            pivot_rows.append(jnp.where(lane >= stop, value, lower[-1]))
        if last < count:
            update = outer_update(jnp.concatenate(upper[first:last], 0), jnp.concatenate(pivot_rows, 0))
            inside = (lane >= start) & (lane < stop)
            for s in range(last, count):
                rows = slice(s * SUBLANES, (s + 1) * SUBLANES)
                tiles[s] = jnp.where(inside, 0.0, tiles[s]) - update[rows]
    return jnp.concatenate(upper, 0), jnp.concatenate(lower, 0)


def row_blocks(matrix):
    return [matrix[i : i + SUBLANES] for i in range(0, matrix.shape[0], SUBLANES)]


def final_kernel(
    row_total, core_ref, own_ref, other_ref, panel_hbm, trailing_hbm, q_hbm, r_ref, p_ref, u_hbm,
    panel_ref, trailing_ref, q_ref, u_ref, in_sems, out_sems,
):
    copies_in = [
        pltpu.make_async_copy(panel_hbm, panel_ref, in_sems.at[0]),
        pltpu.make_async_copy(trailing_hbm, trailing_ref, in_sems.at[1]),
    ]
    for copy in copies_in:
        copy.start()
    rows, order = panel_ref.shape
    inverse_rows = 1.0 / row_total
    swapped = jnp.full(own_ref.shape, core_ref[0], jnp.int32) != 0
    own = own_ref[...] * inverse_rows
    other = other_ref[...] * inverse_rows
    halves = [jnp.where(swapped, other, own), jnp.where(swapped, own, other)]
    quarter = order // 4
    pair_rows = quarter + SUBLANES
    pick = lambda at: unpack_symmetric(
        jnp.concatenate([half[at : at + quarter] for half in halves], 0),
        halves[0][at + quarter : at + pair_rows],
    )
    high = pick(0)
    low = pick(pair_rows)
    cross = jnp.concatenate([half[2 * pair_rows :] for half in halves], 1)
    high_tiles = row_blocks(high)
    first_factor, first_inverse_t = factor_and_inverse(high_tiles)

    peak = jnp.max(jnp.abs(first_factor), axis=0, keepdims=True)
    terms = fixed_point_slices(first_factor, peak, 8, FACTOR_SLICES)
    orders = []
    for size in range(1, FACTOR_SLICES + 1):
        left = jnp.concatenate(terms[:size], 0)
        right = jnp.concatenate(terms[:size][::-1], 0)
        orders.append(exact_product(left, right, (0, 0)))
    remainder, error = two_sum(high, -orders[0])
    remainder, error_next = two_sum(remainder, -orders[1])
    rest = low - orders[2]
    for term in orders[3:]:
        rest = rest - term
    remainder = remainder + ((error + error_next) + rest)
    first_inverse = first_inverse_t.T
    right = bf16_terms(first_inverse, 3)
    near_one = product_of_terms(bf16_terms(first_factor, 3), right)
    carried = product_of_terms(bf16_terms(remainder, 3), right)
    gram_second = product(
        jnp.concatenate([near_one.T, first_inverse_t], 1), jnp.concatenate([near_one, carried], 0)
    )
    second_factor, second_inverse_t = factor_and_inverse(row_blocks(gram_second))

    inverse_t = product(second_inverse_t, first_inverse_t)
    inverse = bf16_terms(inverse_t.T, 3)
    projection = product(inverse_t, cross)
    near_projection = wide(bf16_terms(projection, 2))
    p_ref[...] = projection
    r_ref[...] = product(second_factor, first_factor)
    for copy in copies_in:
        copy.wait()
    copies_out = []
    depth = rows // CHUNKS
    width = projection.shape[1]
    for chunk in range(CHUNKS):
        at = pl.ds(chunk * depth, depth)
        q_factor = product_of_terms(bf16_terms(panel_ref[at, :], 3), inverse)
        q_ref[at, :] = q_factor
        copies_out.append(pltpu.make_async_copy(q_ref.at[at, :], q_hbm.at[at, :], out_sems.at[0, chunk]))
        copies_out[-1].start()
        both = matmul(jnp.concatenate(bf16_terms(q_factor, 2), 1), near_projection)
        u_ref[at, :] = trailing_ref[at, :] - (both[:, width:] + both[:, :width])
        copies_out.append(pltpu.make_async_copy(u_ref.at[at, :], u_hbm.at[at, :], out_sems.at[1, chunk]))
        copies_out[-1].start()
    for copy in copies_out:
        copy.wait()


def all_sum(blocks, pair_rows):
    devices = lax.axis_size(AXES)
    bits = devices.bit_length() - 1
    send = lambda value, mask: lax.ppermute(value, AXES, [(i, i ^ mask) for i in range(devices)])
    add = functools.partial(add_terms, pair_rows=pair_rows)
    odd = lax.axis_index(AXES) % 2
    own = jnp.where(odd == 0, blocks[0], blocks[1])
    value = add(own, send(jnp.where(odd == 0, blocks[1], blocks[0]), 1))
    stages = [(bit,) for bit in range(3, bits)]
    stages.insert(1, (1, 2))
    for stage in stages:
        first = 1 << stage[0]
        if len(stage) == 1:
            value = add(value, send(value, first))
        else:
            second = 1 << stage[1]
            near, far, across = [send(value, mask) for mask in (first, second, first | second)]
            value = add(add(value, near), add(far, across))
    return value, send(value, 1), odd


def on_device(panel, trailing):
    rows, order = panel.shape
    width = trailing.shape[1]
    row_total = float(rows * lax.axis_size(AXES))
    pair_rows = order // 4 + SUBLANES
    local = pl.pallas_call(
        gram_kernel,
        out_shape=pltpu.VMEM((2, 2 * pair_rows + order, order), jnp.float32),
        in_specs=[VMEM] * 2,
        out_specs=VMEM,
    )(panel, trailing)
    own, other, odd = all_sum(local, pair_rows)
    own, other = [pltpu.with_memory_space_constraint(v, pltpu.VMEM) for v in (own, other)]
    shapes = [(rows, order), (order, order), (order, width), (rows, width)]
    far = pl.BlockSpec(memory_space=pltpu.HBM)
    return tuple(
        pl.pallas_call(
            functools.partial(final_kernel, row_total),
            out_shape=[jax.ShapeDtypeStruct(shape, jnp.float32) for shape in shapes],
            in_specs=[pl.BlockSpec(memory_space=pltpu.SMEM), VMEM, VMEM, far, far],
            out_specs=[far, VMEM, VMEM, far],
            scratch_shapes=[
                pltpu.VMEM((rows, order), jnp.float32),
                pltpu.VMEM((rows, width), jnp.float32),
                pltpu.VMEM((rows, order), jnp.float32),
                pltpu.VMEM((rows, width), jnp.float32),
                pltpu.SemaphoreType.DMA((2,)),
                pltpu.SemaphoreType.DMA((2, CHUNKS)),
            ],
        )(odd.astype(jnp.int32).reshape(1), own, other, panel, trailing)
    )


def solution(mesh):
    in_specs = (P(AXES, None), P(AXES, None))
    out_specs = (P(AXES, None), P(), P(), P(AXES, None))
    return jax.shard_map(
        on_device, mesh=mesh, in_specs=in_specs, out_specs=out_specs, check_vma=False
    )
```

```python
import functools

import jax
import jax.numpy as jnp
from jax import lax
from jax.experimental import pallas as pl
from jax.experimental.pallas import tpu as pltpu
from jax.sharding import PartitionSpec as P

AXES = ("wide", "narrow")
SUBLANES = 8
GRAM_SLICES = 5
FACTOR_SLICES = 4
OUTER = 4
CHUNKS = 4
VMEM = pl.BlockSpec(memory_space=pltpu.VMEM)


def matmul(left, right):
    return exact_product(left, right, (1, 0))


def bf16_terms(value, count):
    terms = []
    for _ in range(count):
        term = value.astype(jnp.bfloat16)
        value = value - term.astype(jnp.float32)
        terms.append(term)
    return terms


def wide(right):
    column = jnp.concatenate([right[0], right[1]], 1)
    return jnp.concatenate([column, column], 0)


def product_of_terms(left, right):
    columns = right[0].shape[1]
    small = matmul(jnp.concatenate([left[2], left[0]], 1), jnp.concatenate([right[0], right[2]], 0))
    both = matmul(jnp.concatenate(left[:2], 1), wide(right))
    return (small + both[:, columns:]) + both[:, :columns]


def product(left, right):
    return product_of_terms(bf16_terms(left, 3), bf16_terms(right, 3))


def exact_product(left, right, contract):
    dims = (((contract[0],), (contract[1],)), ((), ()))
    return lax.dot_general(left, right, dims, preferred_element_type=jnp.float32)


def two_sum(left, right):
    total = left + right
    shown = total - left
    return total, (left - (total - shown)) + (right - shown)


def fixed_point_slices(value, peak, first_bits, count):
    sigma = peak * float(2 ** (24 - first_bits))
    terms = []
    for _ in range(count):
        term = (value + sigma) - sigma
        value = value - term
        terms.append(term.astype(jnp.bfloat16))
        sigma = sigma * float(2.0 ** -(first_bits + 1))
    return terms


def gram_kernel(panel_ref, trailing_ref, out_ref):
    panel = panel_ref[...]
    order = panel.shape[1]
    peak = jnp.max(jnp.abs(panel), axis=0, keepdims=True)
    terms = fixed_point_slices(panel, peak, 7, GRAM_SLICES)
    others = bf16_terms(trailing_ref[...], 3)
    width = others[0].shape[1]
    wide_product = lambda left, right: exact_product(left, jnp.concatenate(right, 1), (0, 0))
    zero = wide_product(terms[0], terms + others)
    one = wide_product(terms[1], terms[1:4] + others[:2])
    two = wide_product(terms[2], terms[2:3] + others[:1])
    block = lambda value, i: value[:, i * order : (i + 1) * order]
    rest = (block(zero, 2) + block(one, 1)) + (block(zero, 3) + (block(zero, 4) + block(one, 2)))
    rest = (rest + rest.T) + (block(one, 0) + block(two, 0))
    second, second_low = two_sum(block(zero, 1), block(zero, 1).T)
    high, high_low = two_sum(block(zero, 0), second)
    high, low = two_sum(high, high_low + (second_low + rest))
    part = lambda value, at, i: value[:, at * order + i * width : at * order + (i + 1) * width]
    cross = (part(two, 1, 0) + part(one, 3, 1)) + part(zero, GRAM_SLICES, 2)
    cross = (cross + (part(one, 3, 0) + part(zero, GRAM_SLICES, 1))) + part(zero, GRAM_SLICES, 0)
    high_half, high_rest = pack_symmetric(high)
    low_half, low_rest = pack_symmetric(low)
    half = high_half.shape[0] // 2
    for core in range(2):
        rows = slice(core * half, (core + 1) * half)
        blocks = [high_half[rows], low_half[rows]]
        blocks += [cross[:, core * width // 2 : (core + 1) * width // 2], high_rest[:1], low_rest[:1]]
        at = 0
        for value in blocks:
            out_ref[core, at : at + value.shape[0], :] = value
            at += value.shape[0]


def grid_of(shape):
    return (lax.broadcasted_iota(jnp.int32, shape, d) for d in range(2))


def pack_symmetric(matrix):
    order = matrix.shape[0]
    half = order // 2
    top = matrix[:half]
    bottom = pltpu.roll(matrix[half:], half, 1)
    row, lane = grid_of(top.shape)
    rest = jnp.sum(jnp.where(row == lane, bottom, 0.0), axis=0, keepdims=True)
    return jnp.where(lane < row, bottom, top), jnp.broadcast_to(rest, (SUBLANES, order))


def unpack_symmetric(packed, rest):
    half, order = packed.shape
    turned = packed.T
    left, right = packed[:, :half], packed[:, half:]
    row, lane = grid_of(left.shape)
    diagonal = jnp.broadcast_to(rest[:1, :half], left.shape)
    top = jnp.concatenate([jnp.where(lane >= row, left, turned[:half]), right], 1)
    lower = jnp.where(lane < row, left, jnp.where(lane == row, diagonal, turned[:half]))
    return jnp.concatenate([top, jnp.concatenate([turned[half:], lower], 1)], 0)


def add_terms(left, right, pair_rows):
    high, error = two_sum(left[:pair_rows], right[:pair_rows])
    low = (left[pair_rows : 2 * pair_rows] + right[pair_rows : 2 * pair_rows]) + error
    plain = left[2 * pair_rows : -2] + right[2 * pair_rows : -2]
    rest, error = two_sum(left[-2:-1], right[-2:-1])
    return jnp.concatenate([high, low, plain, rest, (left[-1:] + right[-1:]) + error], 0)


def outer_update(rows, pivots, first):
    left, right = bf16_terms(rows, 3), bf16_terms(pivots, 3)
    left = [left[i] for i in (2, 1, 0, 1, 0, 0)]
    right = [right[i] for i in (0, 1, 2, 0, 1, 0)]
    return matmul(jnp.concatenate(left, 0).T[first:], jnp.concatenate(right, 0))


def factor_and_inverse(tiles, finished=lambda rows: None):
    count = len(tiles)
    shape = tiles[0].shape
    sub, lane = grid_of(shape)
    over_lanes = lambda v, c: jnp.broadcast_to(v[:, c : c + 1], shape)
    over_rows = lambda v, i: jnp.broadcast_to(v[i : i + 1, :], shape)
    tiles = list(tiles)
    upper, lower = [], []
    for first in range(0, count, OUTER):
        last = min(first + OUTER, count)
        size = last - first
        start, stop = first * SUBLANES, last * SUBLANES
        columns = [
            [over_lanes(tiles[first + s], start + c) for c in range(SUBLANES * (s + 1))]
            for s in range(size)
        ]
        pivot_rows = []
        for t in range(size):
            base = start + t * SUBLANES
            current = tiles[first + t]
            inside = (lane >= base) & (lane < base + SUBLANES)
            for s in range(t + 1, size):
                tiles[first + s] = jnp.where(inside, 0.0, tiles[first + s])
            pivots = jnp.zeros(shape, jnp.float32)
            for i in range(SUBLANES):
                k = base + i
                own = t * SUBLANES + i
                pivot = over_rows(columns[t][own], i)
                inverse = 1.0 / pivot
                pivots = jnp.where(sub == i, pivot, pivots)
                row = jnp.where(lane == k, 1.0, over_rows(current, i))
                later = {
                    c: over_rows(columns[c // SUBLANES][own], c % SUBLANES)
                    for c in range(own + 1, SUBLANES * size)
                }
                if i < SUBLANES - 1:
                    column = jnp.where(sub > i, columns[t][own], 0.0) * inverse
                    for c in range(own + 1, SUBLANES * (t + 1)):
                        columns[t][c] = columns[t][c] - column * later[c]
                    current = jnp.where((lane == k) & (sub > i), 0.0, current) - column * row
                if t + 1 < size:
                    below = jnp.where((lane > k) & (lane < base + SUBLANES), 0.0, row)
                    for s in range(t + 1, size):
                        column = columns[s][own] * inverse
                        tiles[first + s] = tiles[first + s] - column * below
                        for c in range(own + 1, SUBLANES * (s + 1)):
                            columns[s][c] = columns[s][c] - column * later[c]
            scale = lax.rsqrt(pivots)
            value = current * scale
            diagonal = sub + base
            upper.append(jnp.where(lane >= diagonal, value, 0.0))
            lower.append(jnp.where(lane < diagonal, value, jnp.where(lane == diagonal, scale, 0.0)))
            pivot_rows.append(jnp.where(lane >= stop, value, lower[-1]))
        finished(jnp.concatenate(upper[first:last], 0))
        if last < count:
            rows = jnp.concatenate(upper[first:last], 0)
            update = outer_update(rows, jnp.concatenate(pivot_rows, 0), stop)
            inside = (lane >= start) & (lane < stop)
            for s in range(last, count):
                at = (s - last) * SUBLANES
                tiles[s] = jnp.where(inside, 0.0, tiles[s]) - update[at : at + SUBLANES]
    return jnp.concatenate(upper, 0), jnp.concatenate(lower, 0)


def row_blocks(matrix):
    return [matrix[i : i + SUBLANES] for i in range(0, matrix.shape[0], SUBLANES)]


def final_kernel(
    row_total, core_ref, own_ref, other_ref, panel_hbm, trailing_hbm, q_hbm, r_ref, p_ref, u_hbm,
    panel_ref, trailing_ref, q_ref, u_ref, in_sems, out_sems,
):
    copies_in = [
        pltpu.make_async_copy(panel_hbm, panel_ref, in_sems.at[0]),
        pltpu.make_async_copy(trailing_hbm, trailing_ref, in_sems.at[1]),
    ]
    for copy in copies_in:
        copy.start()
    rows, order = panel_ref.shape
    inverse_rows = 1.0 / row_total
    swapped = jnp.full(own_ref.shape, core_ref[0], jnp.int32) != 0
    own = own_ref[...] * inverse_rows
    other = other_ref[...] * inverse_rows
    halves = [jnp.where(swapped, other, own), jnp.where(swapped, own, other)]
    quarter = order // 4
    pick = lambda at, row: unpack_symmetric(
        jnp.concatenate([half[at : at + quarter] for half in halves], 0),
        halves[0][row : row + 1],
    )
    high = pick(0, own_ref.shape[0] - 2)
    low = pick(quarter, own_ref.shape[0] - 1)
    cross = jnp.concatenate([half[2 * quarter : -2] for half in halves], 1)

    row, lane = grid_of(high.shape)
    peak = jnp.sqrt(jnp.sum(jnp.where(row == lane, high, 0.0), axis=0, keepdims=True)) * 1.001
    orders = [None] * FACTOR_SLICES

    def add_products(rows):
        terms = fixed_point_slices(rows, peak, 8, FACTOR_SLICES)
        for size in range(1, FACTOR_SLICES + 1):
            left = jnp.concatenate(terms[:size], 0)
            right = jnp.concatenate(terms[:size][::-1], 0)
            value = exact_product(left, right, (0, 0))
            orders[size - 1] = value if orders[size - 1] is None else orders[size - 1] + value

    first_factor, first_inverse_t = factor_and_inverse(row_blocks(high), add_products)

    remainder, error = two_sum(high, -orders[0])
    remainder, error_next = two_sum(remainder, -orders[1])
    rest = low - orders[2]
    for term in orders[3:]:
        rest = rest - term
    remainder = remainder + ((error + error_next) + rest)
    first_inverse = first_inverse_t.T
    right = bf16_terms(first_inverse, 3)
    near_one = product_of_terms(bf16_terms(first_factor, 3), right)
    carried = product_of_terms(bf16_terms(remainder, 3), right)
    gram_second = product(
        jnp.concatenate([near_one.T, first_inverse_t], 1), jnp.concatenate([near_one, carried], 0)
    )
    second_factor, second_inverse_t = factor_and_inverse(row_blocks(gram_second))

    inverse_t = product(second_inverse_t, first_inverse_t)
    inverse = bf16_terms(inverse_t.T, 3)
    projection = product(inverse_t, cross)
    near_projection = wide(bf16_terms(projection, 2))
    p_ref[...] = projection
    r_ref[...] = product(second_factor, first_factor)
    for copy in copies_in:
        copy.wait()
    copies_out = []
    depth = rows // CHUNKS
    width = projection.shape[1]
    for chunk in range(CHUNKS):
        at = pl.ds(chunk * depth, depth)
        q_factor = product_of_terms(bf16_terms(panel_ref[at, :], 3), inverse)
        q_ref[at, :] = q_factor
        copies_out.append(pltpu.make_async_copy(q_ref.at[at, :], q_hbm.at[at, :], out_sems.at[0, chunk]))
        copies_out[-1].start()
        both = matmul(jnp.concatenate(bf16_terms(q_factor, 2), 1), near_projection)
        u_ref[at, :] = trailing_ref[at, :] - (both[:, width:] + both[:, :width])
        copies_out.append(pltpu.make_async_copy(u_ref.at[at, :], u_hbm.at[at, :], out_sems.at[1, chunk]))
        copies_out[-1].start()
    for copy in copies_out:
        copy.wait()


def all_sum(blocks, pair_rows):
    devices = lax.axis_size(AXES)
    bits = devices.bit_length() - 1
    send = lambda value, mask: lax.ppermute(value, AXES, [(i, i ^ mask) for i in range(devices)])
    add = functools.partial(add_terms, pair_rows=pair_rows)
    odd = lax.axis_index(AXES) % 2
    own = jnp.where(odd == 0, blocks[0], blocks[1])
    value = add(own, send(jnp.where(odd == 0, blocks[1], blocks[0]), 1))
    stages = [(bit,) for bit in range(3, bits)]
    stages.insert(1, (1, 2))
    for stage in stages:
        first = 1 << stage[0]
        if len(stage) == 1:
            value = add(value, send(value, first))
        else:
            second = 1 << stage[1]
            near, far, across = [send(value, mask) for mask in (first, second, first | second)]
            value = add(add(value, near), add(far, across))
    return value, send(value, 1), odd


def on_device(panel, trailing):
    rows, order = panel.shape
    width = trailing.shape[1]
    row_total = float(rows * lax.axis_size(AXES))
    pair_rows = order // 4
    local = pl.pallas_call(
        gram_kernel,
        out_shape=pltpu.VMEM((2, 2 * pair_rows + order + 2, order), jnp.float32),
        in_specs=[VMEM] * 2,
        out_specs=VMEM,
    )(panel, trailing)
    own, other, odd = all_sum(local, pair_rows)
    own, other = [pltpu.with_memory_space_constraint(v, pltpu.VMEM) for v in (own, other)]
    shapes = [(rows, order), (order, order), (order, width), (rows, width)]
    far = pl.BlockSpec(memory_space=pltpu.HBM)
    return tuple(
        pl.pallas_call(
            functools.partial(final_kernel, row_total),
            out_shape=[jax.ShapeDtypeStruct(shape, jnp.float32) for shape in shapes],
            in_specs=[pl.BlockSpec(memory_space=pltpu.SMEM), VMEM, VMEM, far, far],
            out_specs=[far, VMEM, VMEM, far],
            scratch_shapes=[
                pltpu.VMEM((rows, order), jnp.float32),
                pltpu.VMEM((rows, width), jnp.float32),
                pltpu.VMEM((rows, order), jnp.float32),
                pltpu.VMEM((rows, width), jnp.float32),
                pltpu.SemaphoreType.DMA((2,)),
                pltpu.SemaphoreType.DMA((2, CHUNKS)),
            ],
        )(odd.astype(jnp.int32).reshape(1), own, other, panel, trailing)
    )


def solution(mesh):
    in_specs = (P(AXES, None), P(AXES, None))
    out_specs = (P(AXES, None), P(), P(), P(AXES, None))
    return jax.shard_map(
        on_device, mesh=mesh, in_specs=in_specs, out_specs=out_specs, check_vma=False
    )
```
